256 devices in a mesh: proj: 16 (over x, y_lo, core), tile: 16 (over z, y_hi).
Axes of the slice: x: 4, y: 4 (y_hi: 2, y_lo: 2; y = y_hi * 2 + y_lo), z: 8, core: 2. Of those that a mesh axis runs over, the one named last changes fastest.
Arguments:
- raw: bfloat16 [32, 1024, 4096], P(None, 'proj', 'tile'), may hold values from -6 to 6
- row_weights: bfloat16 [32, 16, 128, 256], P('proj', 'tile'), may hold values from 0 to 1
- col_weights: bfloat16 [32, 16, 1024, 2048], P('proj', 'tile'), may hold values from 0 to 1
- band_start: int32 [32, 16], replicated, may hold values from 0 to 768
- band_length: int32 [32, 16], replicated, may hold values from 64 to 256, as said below
- col_offset: int32 [32, 16], P('proj', 'tile'), may hold values from 0 to 24
Outputs:
- slab: float32 [128, 32768], P('proj', 'tile')
The draws below stay inside these ranges and needn't reach their ends.
Inputs may be any that keep to these rules, and one draw needn't show every extreme that they name: `band_length`: in every projection some tile uses exactly 256 rows.
All inputs are finite; a program needn't handle non-finite values.
Results may differ from the reference program's by a relative error of at most 0.008.
Values may be sent and summed in bfloat16 or wider, within the bound.
No kernel may reach another device: no remote copies, remote signals or barrier semaphores. Data moves between devices by JAX's collectives and lax.ppermute only.
A program may use at most 128 MiB of HBM per device.

```python
import math
import jax
import jax.numpy as jnp
from jax import lax

DU = 4096
BAND = 1024
LMAX = 256
CW = 1024
SLICES = 128
VT = 2048
P_SIZE = 32
TILES = 16


def draw_band_length(key, part):
    key = jax.random.fold_in(key, 11)
    first, second = jax.random.split(key)
    base = jax.random.randint(first, (P_SIZE, TILES), LMAX // 4, LMAX + 1)
    pick = jax.random.randint(second, (P_SIZE,), 0, TILES)
    full = jnp.arange(TILES, dtype=jnp.int32)[None, :] == pick[:, None]
    return jnp.where(full, LMAX, base).astype(jnp.int32)


def draw_row_weights(key, part):
    key = jax.random.fold_in(key, 21)
    first, second = jax.random.split(key)
    jitter = jax.random.uniform(first, (P_SIZE, TILES, 1, 1), jnp.float32, -LMAX / 8.0, LMAX / 8.0)
    center = (jnp.arange(SLICES, dtype=jnp.float32) + 0.5)[None, None, :, None] * (LMAX / SLICES) + jitter
    gap = jnp.abs(jnp.arange(LMAX, dtype=jnp.float32)[None, None, None, :] - center)
    spread_width = 2.0
    hat = jnp.maximum(0.0, 1.0 - gap / spread_width) / spread_width
    rough = jax.random.uniform(second, (P_SIZE, TILES, SLICES, LMAX), jnp.float32, 0.5, 1.5)
    return (hat * rough).astype(jnp.bfloat16)


def draw_col_weights(key, part):
    key = jax.random.fold_in(key, 31)
    first, second = jax.random.split(key)
    jitter = jax.random.uniform(first, (P_SIZE, TILES, 1, 1), jnp.float32, -CW / 16.0, CW / 16.0)
    center = (jnp.arange(VT, dtype=jnp.float32) + 0.5)[None, None, None, :] * (CW / VT) + jitter
    gap = jnp.abs(jnp.arange(CW, dtype=jnp.float32)[None, None, :, None] - center)
    spread_width = max(2.0, 2.0 * CW / VT)
    hat = jnp.maximum(0.0, 1.0 - gap / spread_width) / spread_width
    rough = jax.random.uniform(second, (P_SIZE, TILES, CW, VT), jnp.float32, 0.5, 1.5)
    return (hat * rough).astype(jnp.bfloat16)


def touch_ends(array, key, least, top_value):
    longest = array.shape.index(max(array.shape))
    spots = []
    for shift in (0, 1):
        where = [jax.random.randint(jax.random.fold_in(key, axis), (), 0, length) for axis, length in enumerate(array.shape)]
        where[longest] = (where[longest] + shift) % array.shape[longest]
        spots.append(tuple(where))
    return array.at[spots[0]].set(least).at[spots[1]].set(top_value)


def block_scale(key, shape, cuts, smallest, top_value):
    loudness, own = 1.0, jax.random.fold_in(key, 6)
    for axis_at, blocks in cuts:
        draws = jnp.exp(jax.random.uniform(jax.random.fold_in(own, axis_at), (blocks,), jnp.float32, smallest / len(cuts), top_value / len(cuts)))
        loudness = loudness * jnp.repeat(draws, shape[axis_at] // blocks).reshape([-1 if axis == axis_at else 1 for axis in range(len(shape))])
    return loudness


def noise(key, dims, scale, reach, pieces=(), held_as=jnp.bfloat16):
    factor_of = block_scale(key, dims, pieces, -0.22, 0.18) if pieces else 1.0
    array = jax.random.normal(key, dims, jnp.float32) * scale * factor_of
    return jnp.minimum(jnp.maximum(array, -reach), reach).astype(held_as)


def setup_inputs(seed: int = 0) -> dict:
    streams_of = jax.random.split(jax.random.key(seed), 7)
    return {
        "raw": noise(streams_of[0], (P_SIZE, BAND, DU), 1.0, 6.0, ((1, 16), (2, 16))),
        "row_weights": draw_row_weights(jax.random.fold_in(streams_of[6], 71), 0),
        "col_weights": draw_col_weights(jax.random.fold_in(streams_of[6], 71), 0),
        "band_start": touch_ends(jax.random.randint(streams_of[3], (P_SIZE, TILES), 0, BAND - LMAX + 1), jax.random.fold_in(streams_of[3], 1), 0, BAND - LMAX).astype(jnp.int32),
        "band_length": draw_band_length(jax.random.fold_in(streams_of[6], 71), 0),
        "col_offset": touch_ends(jax.random.randint(streams_of[5], (P_SIZE, TILES), 0, DU // 128 - CW // 128 + 1), jax.random.fold_in(streams_of[5], 1), 0, (DU // 128 - CW // 128 + 1) - 1).astype(jnp.int32),
    }


def tap_tiles():
    rows_a = jnp.arange(128, dtype=jnp.int32)[:, None]
    cols_c = jnp.arange(128, dtype=jnp.int32)[None, :]
    tiles = []
    for shift in (-1, 0, 1):
        offset = cols_c - rows_a - 128 * shift
        offset_f = offset.astype(jnp.float32)
        odd_mask = offset % 2 != 0
        safe_sq = jnp.where(offset == 0, 1.0, offset_f * offset_f)
        value = jnp.where(offset == 0, 0.25, jnp.where(odd_mask, -1.0 / (math.pi * math.pi * safe_sq), 0.0))
        value = jnp.where((offset >= -128) & (offset <= 127), value, 0.0)
        tiles.append(value.astype(jnp.bfloat16))
    return tiles

def cos_weight(rows, cols, total_rows, total_cols):
    dist = 2.0 * total_cols
    vcoord = rows.astype(jnp.float32) + 0.5 - total_rows / 2.0
    ucoord = cols.astype(jnp.float32) + 0.5 - total_cols / 2.0
    return dist / jnp.sqrt(dist * dist + ucoord[None, :] ** 2 + vcoord[:, None] ** 2)

def filter_one(proj_rows, tiles):
    rows_n, cols_n = proj_rows.shape
    weight = cos_weight(jnp.arange(rows_n, dtype=jnp.int32), jnp.arange(cols_n, dtype=jnp.int32), rows_n, cols_n)
    weighted = (proj_rows.astype(jnp.float32) * weight).astype(jnp.bfloat16)
    padded = jnp.pad(weighted, ((0, 0), (128, 128)))
    total = jnp.zeros((rows_n, cols_n // 128, 128), jnp.float32)
    for index in range(3):
        piece = padded[:, 128 * index:128 * index + cols_n].reshape(rows_n, cols_n // 128, 128)
        total = total + jnp.einsum('rna,ab->rnb', piece.astype(jnp.float32), tiles[index].astype(jnp.float32), precision=lax.Precision.HIGHEST)
    return total.reshape(rows_n, cols_n).astype(jnp.bfloat16)

def reference(raw, row_weights, col_weights, band_start, band_length, col_offset):
    tiles = tap_tiles()
    filtered = lax.map(lambda x: filter_one(x, tiles), raw)

    def one_pair(proj_data, rw, cw, start, length, offset):
        rows = lax.dynamic_slice_in_dim(proj_data, start, LMAX, 0)
        mask = jnp.arange(LMAX, dtype=jnp.int32)[:, None] < length
        rows = jnp.where(mask, rows, jnp.zeros_like(rows))
        window = lax.dynamic_slice_in_dim(rows, offset * 128, CW, 1)
        spread = jnp.dot(window.astype(jnp.float32), cw.astype(jnp.float32), precision=lax.Precision.HIGHEST).astype(jnp.bfloat16)
        return jnp.dot(rw.astype(jnp.float32), spread.astype(jnp.float32), precision=lax.Precision.HIGHEST)

    def step(acc, items):
        proj_data, rw, cw, start, length, offset = items
        terms = jax.vmap(one_pair, in_axes=(None, 0, 0, 0, 0, 0))(proj_data, rw, cw, start, length, offset)
        return (acc + terms, None)
    init = jnp.zeros((TILES, SLICES, VT), jnp.float32)
    acc, _ = lax.scan(step, init, (filtered, row_weights, col_weights, band_start, band_length, col_offset))
    return jnp.transpose(acc, (1, 0, 2)).reshape(SLICES, TILES * VT)
```

```python
import math

import jax
import jax.numpy as jnp
from jax import lax
from jax.experimental import pallas as pl
from jax.experimental.pallas import tpu as pltpu
from jax.sharding import PartitionSpec as P

LMAX = 256
TAP_REACH = 128
BF16 = jnp.bfloat16


def tap_matrix(width):
    rows = jnp.arange(width + 2 * TAP_REACH, dtype=jnp.int32)[:, None]
    cols = jnp.arange(width, dtype=jnp.int32)[None, :]
    offset = cols - rows + TAP_REACH
    offset_f = offset.astype(jnp.float32)
    safe_sq = jnp.where(offset == 0, 1.0, offset_f * offset_f)
    value = jnp.where(
        offset == 0, 0.25, jnp.where(offset % 2 != 0, -1.0 / (math.pi * math.pi * safe_sq), 0.0)
    )
    value = jnp.where((offset >= -TAP_REACH) & (offset < TAP_REACH), value, 0.0)
    return value.astype(BF16)


def gather_offsets(offsets, me_count):
    flat = offsets.reshape(-1)
    bit = 1
    while bit < me_count:
        flat = jnp.concatenate(
            [flat, lax.ppermute(flat, "tile", [(i, i ^ bit) for i in range(me_count)])]
        )
        bit *= 2
    return flat


def filter_cut(info_ref, recv_ref, weight_ref, taps_ref, out_ref, padded, filtered):
    groups, n_src, chunk, width = recv_ref.shape
    n_tile, rows_out, win = out_ref.shape
    periods = rows_out // chunk
    rows = groups * chunk
    total = n_src * width
    me = info_ref[2 * n_tile]
    row_class = info_ref[2 * n_tile + 1]
    zero = jnp.zeros((rows, TAP_REACH), BF16)
    padded[:, :TAP_REACH] = zero
    padded[:, TAP_REACH + total :] = zero
    for src in range(n_src):
        piece = recv_ref[:, src].astype(jnp.float32)
        piece = piece * weight_ref[:, :, width * src : width * (src + 1)]
        lo = TAP_REACH + width * src
        padded[:, lo : lo + width] = piece.reshape(rows, width).astype(BF16)
    for src in range(n_src):
        lo = width * src
        block = jnp.dot(
            padded[:, lo : lo + width + 2 * TAP_REACH],
            taps_ref[...],
            preferred_element_type=jnp.float32,
        )
        filtered[:, :, lo : lo + width] = block.reshape(groups, chunk, width)
    row_ids = lax.broadcasted_iota(jnp.int32, (chunk, win), 0)
    span = chunk * 8

    @pl.loop(0, n_tile)
    def _(k):
        start = info_ref[k]
        col = pl.multiple_of(info_ref[n_tile + k] * 128, 128)
        tile = jnp.bitwise_xor(me, k)
        parts = []
        for m in range(periods):
            delta = start - (span * m + chunk * row_class) + LMAX
            low = lax.shift_right_logical(delta, 8)
            rest = jnp.bitwise_and(delta, LMAX - 1)
            first = jnp.clip(low - 1, 0, groups // periods - 1) * periods + m
            second = jnp.clip(low, 0, groups // periods - 1) * periods + m
            parts.append(
                jnp.where(
                    row_ids >= rest,
                    filtered[first, :, pl.ds(col, win)],
                    filtered[second, :, pl.ds(col, win)],
                )
            )
        out_ref[tile] = jnp.concatenate(parts, axis=0).astype(BF16)


def spread_sum(recv_ref, rowm_ref, colw_ref, out_ref):
    n_src, rows, win = recv_ref.shape
    local = rowm_ref.shape[0]
    per = n_src // local
    acc = None
    for q in range(local):
        window = recv_ref[per * q : per * (q + 1)].reshape(per * rows, win)
        spread = jnp.dot(window, colw_ref[q, 0], preferred_element_type=jnp.float32).astype(BF16)
        term = jnp.dot(rowm_ref[q], spread, preferred_element_type=jnp.float32)
        acc = term if acc is None else acc + term
    out_ref[...] = acc.reshape(out_ref.shape).astype(BF16)


def body(raw, row_weights, col_weights, band_start, band_length, col_offset):
    proj_count, rows_dev, cols_dev = raw.shape
    n_proj = lax.axis_size("proj")
    n_tile = lax.axis_size("tile")
    proj_me = lax.axis_index("proj")
    tile_me = lax.axis_index("tile")
    local = proj_count // n_proj
    total_rows = rows_dev * n_proj
    total_cols = cols_dev * n_tile
    classes = n_tile // local
    chunk = rows_dev // classes
    slices, vox = row_weights.shape[2], col_weights.shape[3]
    win = col_weights.shape[2]
    rows_out = LMAX // classes

    recv = lax.all_to_all(
        raw.reshape(n_proj * n_tile, chunk, cols_dev),
        ("proj", "tile"),
        split_axis=0,
        concat_axis=0,
        tiled=True,
    ).reshape(n_proj, n_tile, chunk, cols_dev)

    offsets = gather_offsets(col_offset, n_tile).reshape(n_tile, local)
    which = tile_me // classes
    row_class = tile_me % classes
    first_proj = proj_me * local
    starts_all = lax.dynamic_slice(band_start, (first_proj, 0), (local, n_tile))
    lengths_all = lax.dynamic_slice(band_length, (first_proj, 0), (local, n_tile))
    order = jnp.bitwise_xor(jnp.arange(n_tile, dtype=jnp.int32), tile_me)
    my_starts = jnp.take(lax.dynamic_index_in_dim(starts_all, which, 0, False), order)
    my_offsets = lax.dynamic_index_in_dim(offsets, which, 1, False)
    info = jnp.concatenate(
        [my_starts, my_offsets, tile_me.reshape(1), row_class.reshape(1)]
    ).astype(jnp.int32)

    dist = 2.0 * total_cols
    row_ids = (
        rows_dev * jnp.arange(n_proj, dtype=jnp.int32)[:, None]
        + chunk * row_class
        + jnp.arange(chunk, dtype=jnp.int32)[None, :]
    ).astype(jnp.float32)
    vcoord = row_ids + 0.5 - total_rows / 2.0
    ucoord = jnp.arange(total_cols, dtype=jnp.int32).astype(jnp.float32) + 0.5 - total_cols / 2.0
    weight = dist / jnp.sqrt(dist * dist + ucoord[None, None, :] ** 2 + vcoord[:, :, None] ** 2)

    cut = pl.pallas_call(
        filter_cut,
        out_shape=jax.ShapeDtypeStruct((n_tile, rows_out, win), BF16),
        in_specs=[pl.BlockSpec(memory_space=pltpu.SMEM)]
        + [pl.BlockSpec(memory_space=pltpu.VMEM)] * 3,
        out_specs=pl.BlockSpec(memory_space=pltpu.VMEM),
        scratch_shapes=[
            pltpu.VMEM((n_proj * chunk, total_cols + 2 * TAP_REACH), BF16),
            pltpu.VMEM((n_proj, chunk, total_cols), jnp.float32),
        ],
        compiler_params=pltpu.CompilerParams(vmem_limit_bytes=24 << 20),
    )(info, recv, weight, tap_matrix(cols_dev))

    windows = lax.all_to_all(cut, "tile", split_axis=0, concat_axis=0, tiled=True)

    place = jnp.arange(LMAX, dtype=jnp.int32)
    row_mod = place // rows_out * chunk + place % rows_out // chunk * rows_dev + place % chunk
    my_start = lax.dynamic_slice_in_dim(starts_all, tile_me, 1, 1)
    my_length = lax.dynamic_slice_in_dim(lengths_all, tile_me, 1, 1)
    band_row = jnp.bitwise_and(row_mod[None, :] - my_start, LMAX - 1)
    pick = (place[None, :, None] == band_row[:, None, :]) & (band_row < my_length)[:, None, :]
    row_moved = jnp.einsum(
        "qsi,qik->qsk", row_weights[:, 0], pick.astype(BF16), preferred_element_type=jnp.float32
    ).astype(BF16)

    step = 512
    part = pl.pallas_call(
        spread_sum,
        out_shape=jax.ShapeDtypeStruct((n_proj, slices // n_proj, vox), BF16),
        grid=(vox // step,),
        in_specs=[
            pl.BlockSpec((n_tile, rows_out, win), lambda n: (0, 0, 0)),
            pl.BlockSpec((local, slices, LMAX), lambda n: (0, 0, 0)),
            pl.BlockSpec((local, 1, win, step), lambda n: (0, 0, 0, n)),
        ],
        out_specs=pl.BlockSpec((n_proj, slices // n_proj, step), lambda n: (0, 0, n)),
        compiler_params=pltpu.CompilerParams(vmem_limit_bytes=24 << 20),
    )(windows, row_moved, col_weights)

    terms = lax.all_to_all(part, "proj", split_axis=0, concat_axis=0, tiled=True)
    return jnp.sum(terms.astype(jnp.float32), axis=0)


def solution(mesh):
    return jax.shard_map(
        body,
        mesh=mesh,
        in_specs=(
            P(None, "proj", "tile"),
            P("proj", "tile", None, None),
            P("proj", "tile", None, None),
            P(),
            P(),
            P("proj", "tile"),
        ),
        out_specs=P("proj", "tile"),
        check_vma=False,
    )
```

```python
import functools
import math

import jax
import jax.numpy as jnp
from jax import lax
from jax.experimental import pallas as pl
from jax.experimental.pallas import tpu as pltpu
from jax.sharding import PartitionSpec as P

LMAX = 256
TAP_REACH = 128
BF16 = jnp.bfloat16


def tap_matrix(width):
    rows = jnp.arange(width + 2 * TAP_REACH, dtype=jnp.int32)[:, None]
    cols = jnp.arange(width, dtype=jnp.int32)[None, :]
    offset = cols - rows + TAP_REACH
    offset_f = offset.astype(jnp.float32)
    safe_sq = jnp.where(offset == 0, 1.0, offset_f * offset_f)
    value = jnp.where(
        offset == 0, 0.25, jnp.where(offset % 2 != 0, -1.0 / (math.pi * math.pi * safe_sq), 0.0)
    )
    value = jnp.where((offset >= -TAP_REACH) & (offset < TAP_REACH), value, 0.0)
    return value.astype(BF16)


def gather_offsets(offsets, count):
    flat = offsets.reshape(-1)
    far = [flat]
    for k in range(1, count // 4):
        far.append(lax.ppermute(flat, "tile", [(i, (i - 4 * k) % count) for i in range(count)]))
    held = jnp.concatenate(far)
    near = [lax.ppermute(held, "tile", [(i, i ^ m) for i in range(count)]) for m in range(1, 4)]
    return jnp.concatenate([held] + near)


def filter_cut(
    local,
    start_ref,
    off_ref,
    recv_ref,
    weight_hbm,
    taps_ref,
    out_ref,
    padded,
    filtered,
    cut,
    sems,
    weight_ref,
    weight_sems,
):
    groups, n_src, chunk, width = recv_ref.shape
    n_tile, rows_out, win = out_ref.shape
    periods = rows_out // chunk
    rows = groups * chunk
    total = n_src * width
    me = lax.axis_index("tile")
    classes = n_tile // local
    row_class = lax.rem(me, classes)
    which = lax.div(me, classes)
    proj = lax.axis_index("proj") * local + which
    parts = weight_sems.shape[0]
    span = total // parts
    weight_copies = [
        pltpu.make_async_copy(
            weight_hbm.at[:, :, pl.ds(span * n, span)],
            weight_ref.at[:, :, pl.ds(span * n, span)],
            weight_sems.at[n],
        )
        for n in range(parts)
    ]
    for copy in weight_copies:
        copy.start()
    zero = jnp.zeros((rows, TAP_REACH), BF16)
    padded[:, :TAP_REACH] = zero
    padded[:, TAP_REACH + total :] = zero
    for src in range(n_src):
        if width * src % span == 0:
            weight_copies[width * src // span].wait()
        piece = recv_ref[:, src].astype(jnp.float32)
        piece = piece * weight_ref[:, :, width * src : width * (src + 1)]
        lo = TAP_REACH + width * src
        padded[:, lo : lo + width] = piece.reshape(rows, width).astype(BF16)
    for src in range(n_src):
        lo = width * src
        block = jnp.dot(
            padded[:, lo : lo + width + 2 * TAP_REACH],
            taps_ref[...],
            preferred_element_type=jnp.float32,
        )
        filtered[:, :, lo : lo + width] = block.reshape(groups, chunk, width)
    row_ids = lax.broadcasted_iota(jnp.int32, (chunk, win), 0)
    span = chunk * classes

    def send(tile):
        return pltpu.make_async_copy(cut.at[tile], out_ref.at[tile], sems.at[tile])

    @pl.loop(0, n_tile)
    def _(k):
        tile = lax.rem(jnp.bitwise_xor(me, lax.div(k, 4)) + 4 * lax.rem(k, 4), n_tile)
        start = start_ref[proj, tile]
        col = pl.multiple_of(off_ref[local * k + which] * 128, 128)
        parts = []
        for m in range(periods):
            delta = start - (span * m + chunk * row_class) + LMAX
            low = lax.shift_right_logical(delta, 8)
            rest = jnp.bitwise_and(delta, LMAX - 1)
            first = jnp.clip(low - 1, 0, groups // periods - 1) * periods + m
            second = jnp.clip(low, 0, groups // periods - 1) * periods + m
            parts.append(
                jnp.where(
                    row_ids >= rest,
                    filtered[first, :, pl.ds(col, win)],
                    filtered[second, :, pl.ds(col, win)],
                )
            )
        cut[tile] = jnp.concatenate(parts, axis=0).astype(BF16)
        send(tile).start()

    @pl.loop(0, n_tile)
    def _(k):
        send(k).wait()


def spread_sum(recv_ref, rowm_ref, colw_ref, out_ref, held, sems):
    n_src, rows, win = recv_ref.shape
    local = rowm_ref.shape[0]
    step = held.shape[-1]
    per = n_src // local
    n_step = held.shape[1]

    def fetch(q, n):
        return pltpu.make_async_copy(
            colw_ref.at[q, 0, :, pl.ds(n * step, step)], held.at[q, n], sems.at[q, n]
        )

    for n in range(n_step):
        for q in range(local):
            fetch(q, n).start()
    for n in range(n_step):
        acc = None
        for q in range(local):
            window = recv_ref[per * q : per * (q + 1)].reshape(per * rows, win)
            fetch(q, n).wait()
            spread = jnp.dot(window, held[q, n], preferred_element_type=jnp.float32).astype(BF16)
            term = jnp.dot(rowm_ref[q], spread, preferred_element_type=jnp.float32)
            acc = term if acc is None else acc + term
        out_ref[:, :, step * n : step * (n + 1)] = acc.reshape(
            out_ref.shape[0], out_ref.shape[1], step
        ).astype(BF16)


def body(raw, row_weights, col_weights, band_start, band_length, col_offset):
    proj_count, rows_dev, cols_dev = raw.shape
    n_proj = lax.axis_size("proj")
    n_tile = lax.axis_size("tile")
    proj_me = lax.axis_index("proj")
    tile_me = lax.axis_index("tile")
    local = proj_count // n_proj
    total_rows = rows_dev * n_proj
    total_cols = cols_dev * n_tile
    classes = n_tile // local
    chunk = rows_dev // classes
    slices, vox = row_weights.shape[2], col_weights.shape[3]
    win = col_weights.shape[2]
    rows_out = LMAX // classes

    recv = lax.all_to_all(
        raw.reshape(n_proj * n_tile, chunk, cols_dev),
        ("proj", "tile"),
        split_axis=0,
        concat_axis=0,
        tiled=True,
    ).reshape(n_proj, n_tile, chunk, cols_dev)

    offsets = gather_offsets(col_offset, n_tile)
    row_class = tile_me % classes
    first_proj = proj_me * local
    starts_all = lax.dynamic_slice(band_start, (first_proj, 0), (local, n_tile))
    lengths_all = lax.dynamic_slice(band_length, (first_proj, 0), (local, n_tile))

    dist = 2.0 * total_cols
    row_ids = (
        rows_dev * jnp.arange(n_proj, dtype=jnp.int32)[:, None]
        + chunk * row_class
        + jnp.arange(chunk, dtype=jnp.int32)[None, :]
    ).astype(jnp.float32)
    vcoord = row_ids + 0.5 - total_rows / 2.0
    ucoord = jnp.arange(total_cols, dtype=jnp.int32).astype(jnp.float32) + 0.5 - total_cols / 2.0
    weight = dist / jnp.sqrt(dist * dist + ucoord[None, None, :] ** 2 + vcoord[:, :, None] ** 2)

    cut = pl.pallas_call(
        functools.partial(filter_cut, local),
        out_shape=jax.ShapeDtypeStruct((n_tile, rows_out, win), BF16),
        in_specs=[pl.BlockSpec(memory_space=pltpu.SMEM)] * 2
        + [
            pl.BlockSpec(memory_space=pltpu.VMEM),
            pl.BlockSpec(memory_space=pltpu.HBM),
            pl.BlockSpec(memory_space=pltpu.VMEM),
        ],
        out_specs=pl.BlockSpec(memory_space=pltpu.HBM),
        scratch_shapes=[
            pltpu.VMEM((n_proj * chunk, total_cols + 2 * TAP_REACH), BF16),
            pltpu.VMEM((n_proj, chunk, total_cols), jnp.float32),
            pltpu.VMEM((n_tile, rows_out, win), BF16),
            pltpu.SemaphoreType.DMA((n_tile,)),
            pltpu.VMEM((n_proj, chunk, total_cols), jnp.float32),
            pltpu.SemaphoreType.DMA((4,)),
        ],
        compiler_params=pltpu.CompilerParams(vmem_limit_bytes=50 << 20),
    )(band_start, offsets, recv, weight, tap_matrix(cols_dev))

    windows = lax.all_to_all(cut, "tile", split_axis=0, concat_axis=0, tiled=True)

    place = jnp.arange(LMAX, dtype=jnp.int32)
    row_mod = place // rows_out * chunk + place % rows_out // chunk * rows_dev + place % chunk
    my_start = lax.dynamic_slice_in_dim(starts_all, tile_me, 1, 1)
    my_length = lax.dynamic_slice_in_dim(lengths_all, tile_me, 1, 1)
    band_row = jnp.bitwise_and(row_mod[None, :] - my_start, LMAX - 1)
    pick = (place[None, :, None] == band_row[:, None, :]) & (band_row < my_length)[:, None, :]
    row_moved = jnp.einsum(
        "qsi,qik->qsk", row_weights[:, 0], pick.astype(BF16), preferred_element_type=jnp.float32
    ).astype(BF16)

    step = 512
    part = pl.pallas_call(
        spread_sum,
        out_shape=jax.ShapeDtypeStruct((n_proj, slices // n_proj, vox), BF16),
        in_specs=[
            pl.BlockSpec(memory_space=pltpu.VMEM),
            pl.BlockSpec(memory_space=pltpu.VMEM),
            pl.BlockSpec(memory_space=pltpu.HBM),
        ],
        out_specs=pl.BlockSpec(memory_space=pltpu.VMEM),
        scratch_shapes=[
            pltpu.VMEM((local, vox // step, win, step), BF16),
            pltpu.SemaphoreType.DMA((local, vox // step)),
        ],
        compiler_params=pltpu.CompilerParams(vmem_limit_bytes=48 << 20),
    )(windows, row_moved, col_weights)

    terms = lax.all_to_all(part, "proj", split_axis=0, concat_axis=0, tiled=True)
    return jnp.sum(terms.astype(jnp.float32), axis=0)


def solution(mesh):
    return jax.shard_map(
        body,
        mesh=mesh,
        in_specs=(
            P(None, "proj", "tile"),
            P("proj", "tile", None, None),
            P("proj", "tile", None, None),
            P(),
            P(),
            P("proj", "tile"),
        ),
        out_specs=P("proj", "tile"),
        check_vma=False,
    )
```

```python
import functools
import math

import jax
import jax.numpy as jnp
from jax import lax
from jax.experimental import pallas as pl
from jax.experimental.pallas import tpu as pltpu
from jax.sharding import PartitionSpec as P

LMAX = 256
TAP_REACH = 128
BF16 = jnp.bfloat16


def tap_matrix(width):
    rows = jnp.arange(width + 2 * TAP_REACH, dtype=jnp.int32)[:, None]
    cols = jnp.arange(width, dtype=jnp.int32)[None, :]
    offset = cols - rows + TAP_REACH
    offset_f = offset.astype(jnp.float32)
    safe_sq = jnp.where(offset == 0, 1.0, offset_f * offset_f)
    value = jnp.where(
        offset == 0, 0.25, jnp.where(offset % 2 != 0, -1.0 / (math.pi * math.pi * safe_sq), 0.0)
    )
    value = jnp.where((offset >= -TAP_REACH) & (offset < TAP_REACH), value, 0.0)
    return value.astype(BF16)


def gather_offsets(offsets, count):
    flat = offsets.reshape(-1)
    far = [flat]
    for k in range(1, count // 4):
        far.append(lax.ppermute(flat, "tile", [(i, (i - 4 * k) % count) for i in range(count)]))
    held = jnp.concatenate(far)
    near = [lax.ppermute(held, "tile", [(i, i ^ m) for i in range(count)]) for m in range(1, 4)]
    return jnp.concatenate([held] + near)


def filter_cut(
    local,
    start_ref,
    off_ref,
    recv_ref,
    weight_ref,
    taps_ref,
    out_ref,
    padded,
    filtered,
):
    groups, n_src, chunk, width = recv_ref.shape
    n_tile, rows_out, win = out_ref.shape
    periods = rows_out // chunk
    rows = groups * chunk
    total = n_src * width
    me = lax.axis_index("tile")
    classes = n_tile // local
    row_class = lax.rem(me, classes)
    which = lax.div(me, classes)
    proj = lax.axis_index("proj") * local + which
    zero = jnp.zeros((rows, TAP_REACH), BF16)
    padded[:, :TAP_REACH] = zero
    padded[:, TAP_REACH + total :] = zero
    for src in range(n_src):
        piece = recv_ref[:, src].astype(jnp.float32)
        piece = piece * weight_ref[:, :, width * src : width * (src + 1)]
        lo = TAP_REACH + width * src
        padded[:, lo : lo + width] = piece.reshape(rows, width).astype(BF16)
    for src in range(n_src):
        lo = width * src
        block = jnp.dot(
            padded[:, lo : lo + width + 2 * TAP_REACH],
            taps_ref[...],
            preferred_element_type=jnp.float32,
        )
        filtered[:, :, lo : lo + width] = block.reshape(groups, chunk, width)
    row_ids = lax.broadcasted_iota(jnp.int32, (chunk, win), 0)
    span = chunk * classes

    @pl.loop(0, n_tile)
    def _(k):
        tile = lax.rem(jnp.bitwise_xor(me, lax.div(k, 4)) + 4 * lax.rem(k, 4), n_tile)
        start = start_ref[proj, tile]
        col = pl.multiple_of(off_ref[local * k + which] * 128, 128)
        parts = []
        for m in range(periods):
            delta = start - (span * m + chunk * row_class) + LMAX
            low = lax.shift_right_logical(delta, 8)
            rest = jnp.bitwise_and(delta, LMAX - 1)
            first = jnp.clip(low - 1, 0, groups // periods - 1) * periods + m
            second = jnp.clip(low, 0, groups // periods - 1) * periods + m
            parts.append(
                jnp.where(
                    row_ids >= rest,
                    filtered[first, :, pl.ds(col, win)],
                    filtered[second, :, pl.ds(col, win)],
                )
            )
        out_ref[tile] = jnp.concatenate(parts, axis=0).astype(BF16)


def spread_sum(recv_ref, rowm_ref, colw_ref, out_ref, held, sems):
    n_src, rows, win = recv_ref.shape
    local = rowm_ref.shape[0]
    step = held.shape[-1]
    per = n_src // local
    n_step = held.shape[1]

    def fetch(q, n):
        return pltpu.make_async_copy(
            colw_ref.at[q, 0, :, pl.ds(n * step, step)], held.at[q, n], sems.at[q, n]
        )

    for n in range(n_step):
        for q in range(local):
            fetch(q, n).start()
    for n in range(n_step):
        acc = None
        for q in range(local):
            window = recv_ref[per * q : per * (q + 1)].reshape(per * rows, win)
            fetch(q, n).wait()
            spread = jnp.dot(window, held[q, n], preferred_element_type=jnp.float32).astype(BF16)
            term = jnp.dot(rowm_ref[q], spread, preferred_element_type=jnp.float32)
            acc = term if acc is None else acc + term
        out_ref[:, :, step * n : step * (n + 1)] = acc.reshape(
            out_ref.shape[0], out_ref.shape[1], step
        ).astype(BF16)


def body(raw, row_weights, col_weights, band_start, band_length, col_offset):
    proj_count, rows_dev, cols_dev = raw.shape
    n_proj = lax.axis_size("proj")
    n_tile = lax.axis_size("tile")
    proj_me = lax.axis_index("proj")
    tile_me = lax.axis_index("tile")
    local = proj_count // n_proj
    total_rows = rows_dev * n_proj
    total_cols = cols_dev * n_tile
    classes = n_tile // local
    chunk = rows_dev // classes
    slices, vox = row_weights.shape[2], col_weights.shape[3]
    win = col_weights.shape[2]
    rows_out = LMAX // classes

    recv = lax.all_to_all(
        raw.reshape(n_proj * n_tile, chunk, cols_dev),
        ("proj", "tile"),
        split_axis=0,
        concat_axis=0,
        tiled=True,
    ).reshape(n_proj, n_tile, chunk, cols_dev)

    offsets = gather_offsets(col_offset, n_tile)
    row_class = tile_me % classes
    first_proj = proj_me * local
    starts_all = lax.dynamic_slice(band_start, (first_proj, 0), (local, n_tile))
    lengths_all = lax.dynamic_slice(band_length, (first_proj, 0), (local, n_tile))

    dist = 2.0 * total_cols
    row_ids = (
        rows_dev * jnp.arange(n_proj, dtype=jnp.int32)[:, None]
        + chunk * row_class
        + jnp.arange(chunk, dtype=jnp.int32)[None, :]
    ).astype(jnp.float32)
    vcoord = row_ids + 0.5 - total_rows / 2.0
    ucoord = jnp.arange(total_cols, dtype=jnp.int32).astype(jnp.float32) + 0.5 - total_cols / 2.0
    weight = dist / jnp.sqrt(dist * dist + ucoord[None, None, :] ** 2 + vcoord[:, :, None] ** 2)

    place = jnp.arange(LMAX, dtype=jnp.int32)
    row_mod = place // rows_out * chunk + place % rows_out // chunk * rows_dev + place % chunk
    my_start = lax.dynamic_slice_in_dim(starts_all, tile_me, 1, 1)
    my_length = lax.dynamic_slice_in_dim(lengths_all, tile_me, 1, 1)
    band_row = jnp.bitwise_and(row_mod[None, :] - my_start, LMAX - 1)
    pick = (place[None, :, None] == band_row[:, None, :]) & (band_row < my_length)[:, None, :]
    row_moved = jnp.einsum(
        "qsi,qik->qsk", row_weights[:, 0], pick.astype(BF16), preferred_element_type=jnp.float32
    ).astype(BF16)

    offsets, row_moved = lax.optimization_barrier((offsets, row_moved))
    cut = pl.pallas_call(
        functools.partial(filter_cut, local),
        out_shape=jax.ShapeDtypeStruct((n_tile, rows_out, win), BF16),
        in_specs=[pl.BlockSpec(memory_space=pltpu.SMEM)] * 2
        + [pl.BlockSpec(memory_space=pltpu.VMEM)] * 3,
        out_specs=pl.BlockSpec(memory_space=pltpu.VMEM),
        scratch_shapes=[
            pltpu.VMEM((n_proj * chunk, total_cols + 2 * TAP_REACH), BF16),
            pltpu.VMEM((n_proj, chunk, total_cols), jnp.float32),
        ],
        compiler_params=pltpu.CompilerParams(vmem_limit_bytes=24 << 20),
    )(band_start, offsets, recv, weight, tap_matrix(cols_dev))

    windows = lax.all_to_all(cut, "tile", split_axis=0, concat_axis=0, tiled=True)

    step = 256
    part = pl.pallas_call(
        spread_sum,
        out_shape=jax.ShapeDtypeStruct((n_proj, slices // n_proj, vox), BF16),
        in_specs=[
            pl.BlockSpec(memory_space=pltpu.VMEM),
            pl.BlockSpec(memory_space=pltpu.VMEM),
            pl.BlockSpec(memory_space=pltpu.HBM),
        ],
        out_specs=pl.BlockSpec(memory_space=pltpu.VMEM),
        scratch_shapes=[
            pltpu.VMEM((local, vox // step, win, step), BF16),
            pltpu.SemaphoreType.DMA((local, vox // step)),
        ],
        compiler_params=pltpu.CompilerParams(vmem_limit_bytes=48 << 20),
    )(windows, row_moved, col_weights)

    terms = lax.all_to_all(part, "proj", split_axis=0, concat_axis=0, tiled=True)
    return jnp.sum(terms.astype(jnp.float32), axis=0)


def solution(mesh):
    return jax.shard_map(
        body,
        mesh=mesh,
        in_specs=(
            P(None, "proj", "tile"),
            P("proj", "tile", None, None),
            P("proj", "tile", None, None),
            P(),
            P(),
            P("proj", "tile"),
        ),
        out_specs=P("proj", "tile"),
        check_vma=False,
    )
```

```python
import functools
import math

import jax
import jax.numpy as jnp
from jax import lax
from jax.experimental import pallas as pl
from jax.experimental.pallas import tpu as pltpu
from jax.sharding import PartitionSpec as P

LMAX = 256
TAP_REACH = 128
BF16 = jnp.bfloat16


def tap_matrix(width):
    rows = jnp.arange(width + 2 * TAP_REACH, dtype=jnp.int32)[:, None]
    cols = jnp.arange(width, dtype=jnp.int32)[None, :]
    offset = cols - rows + TAP_REACH
    offset_f = offset.astype(jnp.float32)
    safe_sq = jnp.where(offset == 0, 1.0, offset_f * offset_f)
    value = jnp.where(
        offset == 0, 0.25, jnp.where(offset % 2 != 0, -1.0 / (math.pi * math.pi * safe_sq), 0.0)
    )
    value = jnp.where((offset >= -TAP_REACH) & (offset < TAP_REACH), value, 0.0)
    return value.astype(BF16)


def gather_offsets(offsets, count):
    half = count // 4
    flat = offsets.reshape(-1)
    held = jnp.concatenate([flat, lax.ppermute(flat, "tile", [(i, i ^ 1) for i in range(count)])])
    held = lax.optimization_barrier(held)
    far = [
        lax.ppermute(
            held, "tile", [((i + 2 * (k + half * (i % 2))) % count, i) for i in range(count)]
        )
        for k in range(1, half + 1)
    ]
    return held, jnp.concatenate(far)


def filter_rows(recv_ref, weight_ref, taps_ref, out_ref, padded):
    groups, n_src, chunk, width = recv_ref.shape
    rows = groups * chunk
    total = n_src * width
    zero = jnp.zeros((rows, TAP_REACH), BF16)
    padded[:, :TAP_REACH] = zero
    padded[:, TAP_REACH + total :] = zero
    for src in range(n_src):
        lo = width * src
        piece = recv_ref[:, src].astype(jnp.float32) * weight_ref[:, :, lo : lo + width]
        padded[:, lo + TAP_REACH : lo + TAP_REACH + width] = piece.reshape(rows, width).astype(BF16)
    for src in range(n_src):
        lo = width * src
        block = jnp.dot(
            padded[:, lo : lo + width + 2 * TAP_REACH],
            taps_ref[...],
            preferred_element_type=jnp.float32,
        )
        out_ref[:, :, lo : lo + width] = block.reshape(groups, chunk, width)


def cut_windows(local, start_ref, own_ref, mine_ref, other_ref, filtered, out_ref):
    groups, chunk, _ = filtered.shape
    n_tile, rows_out, win = out_ref.shape
    periods = rows_out // chunk
    me = lax.axis_index("tile")
    classes = n_tile // local
    row_class = lax.rem(me, classes)
    which = lax.div(me, classes)
    proj = lax.axis_index("proj") * local + which
    row_ids = lax.broadcasted_iota(jnp.int32, (chunk, win), 0)
    span = chunk * classes
    half = n_tile // 4
    me_y = lax.rem(me, 2)

    @pl.loop(0, n_tile)
    def _(k):
        turn = lax.div(k, 2)
        y = lax.rem(k, 2)
        side = jnp.where(turn > half, 1, 0)
        near = (jnp.bitwise_xor(y, me_y)) * local + which
        block = jnp.where(turn > half, turn - half, jnp.maximum(turn, 1)) - 1
        spot = (2 * block + jnp.bitwise_xor(y, side)) * local + which
        far = jnp.where(side == me_y, mine_ref[spot], other_ref[spot])
        col = pl.multiple_of(jnp.where(turn == 0, own_ref[near], far) * 128, 128)
        tile = lax.rem(me - me_y + 2 * turn, n_tile) + y
        start = start_ref[tile, proj]
        parts = []
        for m in range(periods):
            delta = start - (span * m + chunk * row_class) + LMAX
            low = lax.shift_right_logical(delta, 8)
            rest = jnp.bitwise_and(delta, LMAX - 1)
            first = jnp.clip(low - 1, 0, groups // periods - 1) * periods + m
            second = jnp.clip(low, 0, groups // periods - 1) * periods + m
            parts.append(
                jnp.where(
                    row_ids >= rest,
                    filtered[first, :, pl.ds(col, win)],
                    filtered[second, :, pl.ds(col, win)],
                )
            )
        out_ref[tile] = jnp.concatenate(parts, axis=0).astype(BF16)


def spread_sum(recv_ref, rowm_ref, colw_ref, out_ref, held, acc, total, sems):
    n_src, rows, win = recv_ref.shape
    local, parts, depth, _ = held.shape
    per = n_src // local

    def fetch(q, k):
        return pltpu.make_async_copy(
            colw_ref.at[q, 0, pl.ds(depth * k, depth)], held.at[q, k], sems.at[q, k]
        )

    for q in range(local):
        for k in range(parts):
            fetch(q, k).start()
    for q in range(local):
        for k in range(parts):
            fetch(q, k).wait()
            window = recv_ref[per * q : per * (q + 1), :, depth * k : depth * (k + 1)]
            piece = jnp.dot(
                window.reshape(per * rows, depth), held[q, k], preferred_element_type=jnp.float32
            )
            if k:
                piece = acc[...] + piece
            if k < parts - 1:
                acc[...] = piece
                continue
            term = jnp.dot(rowm_ref[q], piece.astype(BF16), preferred_element_type=jnp.float32)
            if q:
                term = total[...] + term
            if q < local - 1:
                total[...] = term
            else:
                out_ref[...] = term.reshape(out_ref.shape).astype(BF16)


def body(raw, row_weights, col_weights, band_start, band_length, col_offset):
    proj_count, rows_dev, cols_dev = raw.shape
    n_proj = lax.axis_size("proj")
    n_tile = lax.axis_size("tile")
    proj_me = lax.axis_index("proj")
    tile_me = lax.axis_index("tile")
    local = proj_count // n_proj
    total_rows = rows_dev * n_proj
    total_cols = cols_dev * n_tile
    classes = n_tile // local
    chunk = rows_dev // classes
    slices, vox = row_weights.shape[2], col_weights.shape[3]
    win = col_weights.shape[2]
    rows_out = LMAX // classes

    recv = lax.all_to_all(
        raw.reshape(n_proj * n_tile, chunk, cols_dev),
        ("proj", "tile"),
        split_axis=0,
        concat_axis=0,
        tiled=True,
    ).reshape(n_proj, n_tile, chunk, cols_dev)

    own, mine = gather_offsets(col_offset, n_tile)
    mine, recv = lax.optimization_barrier((mine, recv))
    other = lax.ppermute(mine, "tile", [(i, i ^ 1) for i in range(n_tile)])
    row_class = tile_me % classes
    first_proj = proj_me * local
    starts_all = lax.dynamic_slice(band_start, (first_proj, 0), (local, n_tile))
    lengths_all = lax.dynamic_slice(band_length, (first_proj, 0), (local, n_tile))

    dist = 2.0 * total_cols
    row_ids = (
        rows_dev * jnp.arange(n_proj, dtype=jnp.int32)[:, None]
        + chunk * row_class
        + jnp.arange(chunk, dtype=jnp.int32)[None, :]
    ).astype(jnp.float32)
    vcoord = row_ids + 0.5 - total_rows / 2.0
    ucoord = jnp.arange(total_cols, dtype=jnp.int32).astype(jnp.float32) + 0.5 - total_cols / 2.0
    weight = dist / jnp.sqrt(dist * dist + ucoord[None, None, :] ** 2 + vcoord[:, :, None] ** 2)

    place = jnp.arange(LMAX, dtype=jnp.int32)
    row_mod = place // rows_out * chunk + place % rows_out // chunk * rows_dev + place % chunk
    my_start = lax.dynamic_slice_in_dim(starts_all, tile_me, 1, 1)
    my_length = lax.dynamic_slice_in_dim(lengths_all, tile_me, 1, 1)
    band_row = jnp.bitwise_and(row_mod[None, :] - my_start, LMAX - 1)
    pick = (place[None, :, None] == band_row[:, None, :]) & (band_row < my_length)[:, None, :]
    row_moved = jnp.einsum(
        "qsi,qik->qsk", row_weights[:, 0], pick.astype(BF16), preferred_element_type=jnp.float32
    ).astype(BF16)

    other, row_moved = lax.optimization_barrier((other, row_moved))
    filtered = pl.pallas_call(
        filter_rows,
        out_shape=jax.ShapeDtypeStruct((n_proj, chunk, total_cols), jnp.float32),
        in_specs=[pl.BlockSpec(memory_space=pltpu.VMEM)] * 3,
        out_specs=pl.BlockSpec(memory_space=pltpu.VMEM),
        scratch_shapes=[pltpu.VMEM((n_proj * chunk, total_cols + 2 * TAP_REACH), BF16)],
        compiler_params=pltpu.CompilerParams(vmem_limit_bytes=24 << 20),
    )(recv, weight, tap_matrix(cols_dev))
    cut = pl.pallas_call(
        functools.partial(cut_windows, local),
        out_shape=jax.ShapeDtypeStruct((n_tile, rows_out, win), BF16),
        in_specs=[pl.BlockSpec(memory_space=pltpu.SMEM)] * 4
        + [pl.BlockSpec(memory_space=pltpu.VMEM)],
        out_specs=pl.BlockSpec(memory_space=pltpu.VMEM),
        compiler_params=pltpu.CompilerParams(vmem_limit_bytes=24 << 20),
    )(band_start.T, own, mine, other, filtered)

    windows = lax.all_to_all(cut, "tile", split_axis=0, concat_axis=0, tiled=True)

    parts = 2
    part = pl.pallas_call(
        spread_sum,
        out_shape=jax.ShapeDtypeStruct((n_proj, slices // n_proj, vox), BF16),
        in_specs=[
            pl.BlockSpec(memory_space=pltpu.VMEM),
            pl.BlockSpec(memory_space=pltpu.VMEM),
            pl.BlockSpec(memory_space=pl.ANY),
        ],
        out_specs=pl.BlockSpec(memory_space=pltpu.VMEM),
        scratch_shapes=[
            pltpu.VMEM((local, parts, win // parts, vox), BF16),
            pltpu.VMEM((LMAX, vox), jnp.float32),
            pltpu.VMEM((slices, vox), jnp.float32),
            pltpu.SemaphoreType.DMA((local, parts)),
        ],
        compiler_params=pltpu.CompilerParams(vmem_limit_bytes=48 << 20),
    )(windows, row_moved, col_weights)

    terms = lax.all_to_all(part, "proj", split_axis=0, concat_axis=0, tiled=True)
    return jnp.sum(terms.astype(jnp.float32), axis=0)


def solution(mesh):
    return jax.shard_map(
        body,
        mesh=mesh,
        in_specs=(
            P(None, "proj", "tile"),
            P("proj", "tile", None, None),
            P("proj", "tile", None, None),
            P(),
            P(),
            P("proj", "tile"),
        ),
        out_specs=P("proj", "tile"),
        check_vma=False,
    )
```

```python
import functools
import math

import jax
import jax.numpy as jnp
from jax import lax
from jax.experimental import pallas as pl
from jax.experimental.pallas import tpu as pltpu
from jax.sharding import PartitionSpec as P

LMAX = 256
TAP_REACH = 128
BF16 = jnp.bfloat16


def tap_matrix(width):
    rows = jnp.arange(width + 2 * TAP_REACH, dtype=jnp.int32)[:, None]
    cols = jnp.arange(width, dtype=jnp.int32)[None, :]
    offset = cols - rows + TAP_REACH
    offset_f = offset.astype(jnp.float32)
    safe_sq = jnp.where(offset == 0, 1.0, offset_f * offset_f)
    value = jnp.where(
        offset == 0, 0.25, jnp.where(offset % 2 != 0, -1.0 / (math.pi * math.pi * safe_sq), 0.0)
    )
    value = jnp.where((offset >= -TAP_REACH) & (offset < TAP_REACH), value, 0.0)
    return value.astype(BF16)


def gather_offsets(offsets, count):
    half = count // 4
    flat = offsets.reshape(-1)
    held = jnp.concatenate([flat, lax.ppermute(flat, "tile", [(i, i ^ 1) for i in range(count)])])
    held = lax.optimization_barrier(held)
    far = [
        lax.ppermute(
            held, "tile", [((i + 2 * (k + half * (i % 2))) % count, i) for i in range(count)]
        )
        for k in range(1, half + 1)
    ]
    mine = lax.optimization_barrier(jnp.concatenate(far))
    return held, mine, lax.ppermute(mine, "tile", [(i, i ^ 1) for i in range(count)])


def filter_rows(recv_ref, weight_ref, taps_ref, out_ref, padded):
    groups, n_src, chunk, width = recv_ref.shape
    rows = groups * chunk
    total = n_src * width
    zero = jnp.zeros((rows, TAP_REACH), BF16)
    padded[:, :TAP_REACH] = zero
    padded[:, TAP_REACH + total :] = zero
    for src in range(n_src):
        lo = width * src
        piece = recv_ref[:, src].astype(jnp.float32) * weight_ref[:, :, lo : lo + width]
        padded[:, lo + TAP_REACH : lo + TAP_REACH + width] = piece.reshape(rows, width).astype(BF16)
    for src in range(n_src):
        lo = width * src
        block = jnp.dot(
            padded[:, lo : lo + width + 2 * TAP_REACH],
            taps_ref[...],
            preferred_element_type=jnp.float32,
        )
        out_ref[:, :, lo : lo + width] = block.reshape(groups, chunk, width)


def cut_windows(local, start_ref, own_ref, mine_ref, other_ref, filtered, out_ref):
    groups, chunk, _ = filtered.shape
    n_tile, rows_out, win = out_ref.shape
    periods = rows_out // chunk
    me = lax.axis_index("tile")
    classes = n_tile // local
    row_class = lax.rem(me, classes)
    which = lax.div(me, classes)
    proj = lax.axis_index("proj") * local + which
    row_ids = lax.broadcasted_iota(jnp.int32, (chunk, win), 0)
    span = chunk * classes
    half = n_tile // 4
    me_y = lax.rem(me, 2)

    @pl.loop(0, n_tile)
    def _(k):
        turn = lax.div(k, 2)
        y = lax.rem(k, 2)
        side = jnp.where(turn > half, 1, 0)
        near = (jnp.bitwise_xor(y, me_y)) * local + which
        block = jnp.where(turn > half, turn - half, jnp.maximum(turn, 1)) - 1
        spot = (2 * block + jnp.bitwise_xor(y, side)) * local + which
        far = jnp.where(side == me_y, mine_ref[spot], other_ref[spot])
        col = pl.multiple_of(jnp.where(turn == 0, own_ref[near], far) * 128, 128)
        tile = lax.rem(me - me_y + 2 * turn, n_tile) + y
        start = start_ref[tile, proj]
        parts = []
        for m in range(periods):
            delta = start - (span * m + chunk * row_class) + LMAX
            low = lax.shift_right_logical(delta, 8)
            rest = jnp.bitwise_and(delta, LMAX - 1)
            first = jnp.clip(low - 1, 0, groups // periods - 1) * periods + m
            second = jnp.clip(low, 0, groups // periods - 1) * periods + m
            parts.append(
                jnp.where(
                    row_ids >= rest,
                    filtered[first, :, pl.ds(col, win)],
                    filtered[second, :, pl.ds(col, win)],
                )
            )
        out_ref[tile] = jnp.concatenate(parts, axis=0).astype(BF16)


def spread_sum(recv_ref, rowm_ref, first_ref, colw_ref, out_ref, held, acc, total, sems):
    n_src, rows, win = recv_ref.shape
    local, parts, depth, _ = held.shape
    per = n_src // local

    def fetch(q, k):
        return pltpu.make_async_copy(
            colw_ref.at[q, 0, pl.ds(depth * k, depth)], held.at[q, k], sems.at[q, k]
        )

    for q in range(local):
        for k in range(parts):
            if q:
                fetch(q, k).start()
    for q in range(local):
        for k in range(parts):
            if q:
                fetch(q, k).wait()
            block = held[q, k] if q else first_ref[depth * k : depth * (k + 1)]
            window = recv_ref[per * q : per * (q + 1), :, depth * k : depth * (k + 1)]
            piece = jnp.dot(
                window.reshape(per * rows, depth), block, preferred_element_type=jnp.float32
            )
            if k:
                piece = acc[...] + piece
            if k < parts - 1:
                acc[...] = piece
                continue
            term = jnp.dot(rowm_ref[q], piece.astype(BF16), preferred_element_type=jnp.float32)
            if q:
                term = total[...] + term
            if q < local - 1:
                total[...] = term
            else:
                out_ref[...] = term.reshape(out_ref.shape).astype(BF16)


def body(raw, row_weights, col_weights, band_start, band_length, col_offset):
    proj_count, rows_dev, cols_dev = raw.shape
    n_proj = lax.axis_size("proj")
    n_tile = lax.axis_size("tile")
    proj_me = lax.axis_index("proj")
    tile_me = lax.axis_index("tile")
    local = proj_count // n_proj
    total_rows = rows_dev * n_proj
    total_cols = cols_dev * n_tile
    classes = n_tile // local
    chunk = rows_dev // classes
    slices, vox = row_weights.shape[2], col_weights.shape[3]
    win = col_weights.shape[2]
    rows_out = LMAX // classes

    recv = lax.all_to_all(
        raw.reshape(n_proj * n_tile, chunk, cols_dev),
        ("proj", "tile"),
        split_axis=0,
        concat_axis=0,
        tiled=True,
    ).reshape(n_proj, n_tile, chunk, cols_dev)

    own, mine, other = gather_offsets(col_offset, n_tile)
    row_class = tile_me % classes
    first_proj = proj_me * local
    starts_all = lax.dynamic_slice(band_start, (first_proj, 0), (local, n_tile))
    lengths_all = lax.dynamic_slice(band_length, (first_proj, 0), (local, n_tile))

    dist = 2.0 * total_cols
    row_ids = (
        rows_dev * jnp.arange(n_proj, dtype=jnp.int32)[:, None]
        + chunk * row_class
        + jnp.arange(chunk, dtype=jnp.int32)[None, :]
    ).astype(jnp.float32)
    vcoord = row_ids + 0.5 - total_rows / 2.0
    ucoord = jnp.arange(total_cols, dtype=jnp.int32).astype(jnp.float32) + 0.5 - total_cols / 2.0
    weight = dist / jnp.sqrt(dist * dist + ucoord[None, None, :] ** 2 + vcoord[:, :, None] ** 2)

    place = jnp.arange(LMAX, dtype=jnp.int32)
    row_mod = place // rows_out * chunk + place % rows_out // chunk * rows_dev + place % chunk
    my_start = lax.dynamic_slice_in_dim(starts_all, tile_me, 1, 1)
    my_length = lax.dynamic_slice_in_dim(lengths_all, tile_me, 1, 1)
    band_row = jnp.bitwise_and(row_mod[None, :] - my_start, LMAX - 1)
    pick = (place[None, :, None] == band_row[:, None, :]) & (band_row < my_length)[:, None, :]
    row_moved = jnp.einsum(
        "qsi,qik->qsk", row_weights[:, 0], pick.astype(BF16), preferred_element_type=jnp.float32
    ).astype(BF16)

    parts = 2
    first = col_weights[0, 0]
    other, row_moved, first = lax.optimization_barrier((other, row_moved, first))
    filtered = pl.pallas_call(
        filter_rows,
        out_shape=jax.ShapeDtypeStruct((n_proj, chunk, total_cols), jnp.float32),
        in_specs=[pl.BlockSpec(memory_space=pltpu.VMEM)] * 3,
        out_specs=pl.BlockSpec(memory_space=pltpu.VMEM),
        scratch_shapes=[pltpu.VMEM((n_proj * chunk, total_cols + 2 * TAP_REACH), BF16)],
        compiler_params=pltpu.CompilerParams(vmem_limit_bytes=24 << 20),
    )(recv, weight, tap_matrix(cols_dev))
    cut = pl.pallas_call(
        functools.partial(cut_windows, local),
        out_shape=jax.ShapeDtypeStruct((n_tile, rows_out, win), BF16),
        in_specs=[pl.BlockSpec(memory_space=pltpu.SMEM)] * 4
        + [pl.BlockSpec(memory_space=pltpu.VMEM)],
        out_specs=pl.BlockSpec(memory_space=pltpu.VMEM),
        compiler_params=pltpu.CompilerParams(vmem_limit_bytes=24 << 20),
    )(band_start.T, own, mine, other, filtered)

    windows = lax.all_to_all(cut, "tile", split_axis=0, concat_axis=0, tiled=True)

    part = pl.pallas_call(
        spread_sum,
        out_shape=jax.ShapeDtypeStruct((n_proj, slices // n_proj, vox), BF16),
        in_specs=[
            pl.BlockSpec(memory_space=pltpu.VMEM),
            pl.BlockSpec(memory_space=pltpu.VMEM),
            pl.BlockSpec(memory_space=pltpu.VMEM),
            pl.BlockSpec(memory_space=pl.ANY),
        ],
        out_specs=pl.BlockSpec(memory_space=pltpu.VMEM),
        scratch_shapes=[
            pltpu.VMEM((local, parts, win // parts, vox), BF16),
            pltpu.VMEM((LMAX, vox), jnp.float32),
            pltpu.VMEM((slices, vox), jnp.float32),
            pltpu.SemaphoreType.DMA((local, parts)),
        ],
        compiler_params=pltpu.CompilerParams(vmem_limit_bytes=48 << 20),
    )(windows, row_moved, first, col_weights)

    terms = lax.all_to_all(part, "proj", split_axis=0, concat_axis=0, tiled=True)
    return jnp.sum(terms.astype(jnp.float32), axis=0)


def solution(mesh):
    return jax.shard_map(
        body,
        mesh=mesh,
        in_specs=(
            P(None, "proj", "tile"),
            P("proj", "tile", None, None),
            P("proj", "tile", None, None),
            P(),
            P(),
            P("proj", "tile"),
        ),
        out_specs=P("proj", "tile"),
        check_vma=False,
    )
```

```python
import functools
import math

import jax
import jax.numpy as jnp
from jax import lax
from jax.experimental import pallas as pl
from jax.experimental.pallas import tpu as pltpu
from jax.sharding import PartitionSpec as P

LMAX = 256
TAP_REACH = 128
BF16 = jnp.bfloat16


def tap_matrix(width):
    rows = jnp.arange(width + 2 * TAP_REACH, dtype=jnp.int32)[:, None]
    cols = jnp.arange(width, dtype=jnp.int32)[None, :]
    offset = cols - rows + TAP_REACH
    offset_f = offset.astype(jnp.float32)
    safe_sq = jnp.where(offset == 0, 1.0, offset_f * offset_f)
    value = jnp.where(
        offset == 0, 0.25, jnp.where(offset % 2 != 0, -1.0 / (math.pi * math.pi * safe_sq), 0.0)
    )
    value = jnp.where((offset >= -TAP_REACH) & (offset < TAP_REACH), value, 0.0)
    return value.astype(BF16)


def gather_offsets(offsets, count):
    flat = offsets.reshape(-1)
    held = jnp.concatenate([flat, lax.ppermute(flat, "tile", [(i, i ^ 1) for i in range(count)])])
    held = lax.optimization_barrier(held)

    def fetch(values, turn):
        return lax.ppermute(values, "tile", [((i + 2 * turn) % count, i) for i in range(count)])

    turns = count // 2
    early = [fetch(held, k) for k in range(1, 6)]
    again, early[0] = lax.optimization_barrier((held, early[0]))
    late = [fetch(again, k) for k in range(6, turns)]
    return held, jnp.concatenate(early[:4]), early[4:] + late


def filter_rows(recv_ref, weight_ref, taps_ref, out_ref, padded):
    groups, n_src, chunk, width = recv_ref.shape
    rows = groups * chunk
    total = n_src * width
    zero = jnp.zeros((rows, TAP_REACH), BF16)
    padded[:, :TAP_REACH] = zero
    padded[:, TAP_REACH + total :] = zero
    for src in range(n_src):
        lo = width * src
        piece = recv_ref[:, src].astype(jnp.float32) * weight_ref[:, :, lo : lo + width]
        padded[:, lo + TAP_REACH : lo + TAP_REACH + width] = piece.reshape(rows, width).astype(BF16)
    for src in range(n_src):
        lo = width * src
        block = jnp.dot(
            padded[:, lo : lo + width + 2 * TAP_REACH],
            taps_ref[...],
            preferred_element_type=jnp.float32,
        )
        turns, high, _ = out_ref.shape
        out_ref[:, :, lo : lo + width] = block.reshape(turns, high, width).astype(BF16)


def cut_windows(local, chunk, start_ref, own_ref, next_ref, *refs):
    *late_refs, filtered, out_ref = refs
    turns = filtered.shape[0]
    n_tile, rows_out, win = out_ref.shape
    me = lax.axis_index("tile")
    classes = n_tile // local
    row_class = lax.rem(me, classes)
    which = lax.div(me, classes)
    proj = lax.axis_index("proj") * local + which
    row_ids = lax.broadcasted_iota(jnp.int32, (rows_out, win), 0)
    row_mod = (row_ids // chunk * classes + row_class) * chunk + row_ids % chunk
    me_y = lax.rem(me, 2)

    @pl.loop(0, n_tile)
    def _(k):
        turn = lax.div(k, 2)
        y = lax.rem(k, 2)
        spot = jnp.bitwise_xor(y, me_y) * local + which
        block = own_ref[spot]
        step = 2 * local
        near = n_tile // 2 - 1 - len(late_refs)
        ahead = jnp.clip(turn - 1, 0, near - 1)
        block = jnp.where(turn > 0, next_ref[step * ahead + spot], block)
        for at, late_ref in enumerate(late_refs):
            block = jnp.where(turn == near + 1 + at, late_ref[spot], block)
        col = pl.multiple_of(block * 128, 128)
        tile = lax.rem(me - me_y + 2 * turn, n_tile) + y
        start = start_ref[tile, proj]
        turn_at = lax.shift_right_logical(start, 8)
        later = jnp.minimum(turn_at + 1, turns - 1)
        out_ref[tile] = jnp.where(
            row_mod >= jnp.bitwise_and(start, LMAX - 1),
            filtered[turn_at, :, pl.ds(col, win)],
            filtered[later, :, pl.ds(col, win)],
        )


def spread_sum(recv_ref, rowm_ref, first_ref, colw_ref, out_ref, held, acc, total, sems):
    n_src, rows, win = recv_ref.shape
    local, parts, depth, _ = held.shape
    per = n_src // local

    def fetch(q, k):
        return pltpu.make_async_copy(
            colw_ref.at[q, 0, pl.ds(depth * k, depth)], held.at[q, k], sems.at[q, k]
        )

    for q in range(local):
        for k in range(parts):
            if q:
                fetch(q, k).start()
    for q in range(local):
        for k in range(parts):
            if q:
                fetch(q, k).wait()
            block = held[q, k] if q else first_ref[depth * k : depth * (k + 1)]
            window = recv_ref[per * q : per * (q + 1), :, depth * k : depth * (k + 1)]
            piece = jnp.dot(
                window.reshape(per * rows, depth), block, preferred_element_type=jnp.float32
            )
            if k:
                piece = acc[...] + piece
            if k < parts - 1:
                acc[...] = piece
                continue
            term = jnp.dot(rowm_ref[q], piece.astype(BF16), preferred_element_type=jnp.float32)
            if q:
                term = total[...] + term
            if q < local - 1:
                total[...] = term
            else:
                out_ref[...] = term.reshape(out_ref.shape).astype(BF16)


def body(raw, row_weights, col_weights, band_start, band_length, col_offset):
    proj_count, rows_dev, cols_dev = raw.shape
    n_proj = lax.axis_size("proj")
    n_tile = lax.axis_size("tile")
    proj_me = lax.axis_index("proj")
    tile_me = lax.axis_index("tile")
    local = proj_count // n_proj
    total_rows = rows_dev * n_proj
    total_cols = cols_dev * n_tile
    classes = n_tile // local
    chunk = rows_dev // classes
    slices, vox = row_weights.shape[2], col_weights.shape[3]
    win = col_weights.shape[2]
    rows_out = LMAX // classes

    recv = lax.all_to_all(
        raw.reshape(n_proj * n_tile, chunk, cols_dev),
        ("proj", "tile"),
        split_axis=0,
        concat_axis=0,
        tiled=True,
    ).reshape(n_proj, n_tile, chunk, cols_dev)

    own, ahead, late = gather_offsets(col_offset, n_tile)
    row_class = tile_me % classes
    first_proj = proj_me * local
    starts_all = lax.dynamic_slice(band_start, (first_proj, 0), (local, n_tile))
    lengths_all = lax.dynamic_slice(band_length, (first_proj, 0), (local, n_tile))

    dist = 2.0 * total_cols
    row_ids = (
        rows_dev * jnp.arange(n_proj, dtype=jnp.int32)[:, None]
        + chunk * row_class
        + jnp.arange(chunk, dtype=jnp.int32)[None, :]
    ).astype(jnp.float32)
    vcoord = row_ids + 0.5 - total_rows / 2.0
    ucoord = jnp.arange(total_cols, dtype=jnp.int32).astype(jnp.float32) + 0.5 - total_cols / 2.0
    weight = dist / jnp.sqrt(dist * dist + ucoord[None, None, :] ** 2 + vcoord[:, :, None] ** 2)

    place = jnp.arange(LMAX, dtype=jnp.int32)
    row_mod = place // rows_out * chunk + place % rows_out // chunk * rows_dev + place % chunk
    my_start = lax.dynamic_slice_in_dim(starts_all, tile_me, 1, 1)
    my_length = lax.dynamic_slice_in_dim(lengths_all, tile_me, 1, 1)
    band_row = jnp.bitwise_and(row_mod[None, :] - my_start, LMAX - 1)
    pick = (place[None, :, None] == band_row[:, None, :]) & (band_row < my_length)[:, None, :]
    row_moved = jnp.einsum(
        "qsi,qik->qsk", row_weights[:, 0], pick.astype(BF16), preferred_element_type=jnp.float32
    ).astype(BF16)

    parts = 2
    first = col_weights[0, 0]
    own, row_moved, first = lax.optimization_barrier((own, row_moved, first))
    filtered = pl.pallas_call(
        filter_rows,
        out_shape=jax.ShapeDtypeStruct((total_rows // LMAX, rows_out, total_cols), BF16),
        in_specs=[pl.BlockSpec(memory_space=pltpu.VMEM)] * 3,
        out_specs=pl.BlockSpec(memory_space=pltpu.VMEM),
        scratch_shapes=[pltpu.VMEM((n_proj * chunk, total_cols + 2 * TAP_REACH), BF16)],
        compiler_params=pltpu.CompilerParams(vmem_limit_bytes=24 << 20),
    )(recv, weight, tap_matrix(cols_dev))
    cut = pl.pallas_call(
        functools.partial(cut_windows, local, chunk),
        out_shape=jax.ShapeDtypeStruct((n_tile, rows_out, win), BF16),
        in_specs=[pl.BlockSpec(memory_space=pltpu.SMEM)] * (3 + len(late))
        + [pl.BlockSpec(memory_space=pltpu.VMEM)],
        out_specs=pl.BlockSpec(memory_space=pltpu.VMEM),
        compiler_params=pltpu.CompilerParams(vmem_limit_bytes=24 << 20),
    )(band_start.T, own, ahead, *late, filtered)

    windows = lax.all_to_all(cut, "tile", split_axis=0, concat_axis=0, tiled=True)

    part = pl.pallas_call(
        spread_sum,
        out_shape=jax.ShapeDtypeStruct((n_proj, slices // n_proj, vox), BF16),
        in_specs=[
            pl.BlockSpec(memory_space=pltpu.VMEM),
            pl.BlockSpec(memory_space=pltpu.VMEM),
            pl.BlockSpec(memory_space=pltpu.VMEM),
            pl.BlockSpec(memory_space=pl.ANY),
        ],
        out_specs=pl.BlockSpec(memory_space=pltpu.VMEM),
        scratch_shapes=[
            pltpu.VMEM((local, parts, win // parts, vox), BF16),
            pltpu.VMEM((LMAX, vox), jnp.float32),
            pltpu.VMEM((slices, vox), jnp.float32),
            pltpu.SemaphoreType.DMA((local, parts)),
        ],
        compiler_params=pltpu.CompilerParams(vmem_limit_bytes=48 << 20),
    )(windows, row_moved, first, col_weights)

    terms = lax.all_to_all(part, "proj", split_axis=0, concat_axis=0, tiled=True)
    return jnp.sum(terms.astype(jnp.float32), axis=0)


def solution(mesh):
    return jax.shard_map(
        body,
        mesh=mesh,
        in_specs=(
            P(None, "proj", "tile"),
            P("proj", "tile", None, None),
            P("proj", "tile", None, None),
            P(),
            P(),
            P("proj", "tile"),
        ),
        out_specs=P("proj", "tile"),
        check_vma=False,
    )
```

```python
import functools
import math

import jax
import jax.numpy as jnp
from jax import lax
from jax.experimental import pallas as pl
from jax.experimental.pallas import tpu as pltpu
from jax.sharding import PartitionSpec as P

LMAX = 256
TAP_REACH = 128
BF16 = jnp.bfloat16


def tap_matrix(width):
    rows = jnp.arange(width + 2 * TAP_REACH, dtype=jnp.int32)[:, None]
    cols = jnp.arange(width, dtype=jnp.int32)[None, :]
    offset = cols - rows + TAP_REACH
    offset_f = offset.astype(jnp.float32)
    safe_sq = jnp.where(offset == 0, 1.0, offset_f * offset_f)
    value = jnp.where(
        offset == 0, 0.25, jnp.where(offset % 2 != 0, -1.0 / (math.pi * math.pi * safe_sq), 0.0)
    )
    value = jnp.where((offset >= -TAP_REACH) & (offset < TAP_REACH), value, 0.0)
    return value.astype(BF16)


def gather_offsets(offsets, count):
    flat = offsets.reshape(-1)
    held = jnp.concatenate([flat, lax.ppermute(flat, "tile", [(i, i ^ 1) for i in range(count)])])
    held = lax.optimization_barrier(held)

    def fetch(values, turn):
        return lax.ppermute(values, "tile", [((i + 2 * turn) % count, i) for i in range(count)])

    turns = count // 2
    early = [fetch(held, k) for k in range(1, 6)]
    again, early[0] = lax.optimization_barrier((held, early[0]))
    late = [fetch(again, k) for k in range(6, turns)]
    return held, jnp.concatenate(early[:4]), early[4:] + late


def filter_rows(recv_ref, weight_ref, taps_ref, out_ref, padded):
    groups, n_src, chunk, width = recv_ref.shape
    rows = groups * chunk
    total = n_src * width
    zero = jnp.zeros((rows, TAP_REACH), BF16)
    padded[:, :TAP_REACH] = zero
    padded[:, TAP_REACH + total :] = zero
    for src in range(n_src):
        lo = width * src
        piece = recv_ref[:, src].astype(jnp.float32) * weight_ref[:, :, lo : lo + width]
        padded[:, lo + TAP_REACH : lo + TAP_REACH + width] = piece.reshape(rows, width).astype(BF16)
    for src in range(n_src):
        lo = width * src
        block = jnp.dot(
            padded[:, lo : lo + width + 2 * TAP_REACH],
            taps_ref[...],
            preferred_element_type=jnp.float32,
        )
        turns, high, _ = out_ref.shape
        out_ref[:, :, lo : lo + width] = block.reshape(turns, high, width).astype(BF16)


def cut_windows(local, chunk, start_ref, own_ref, next_ref, *refs):
    *late_refs, filtered, out_ref, table = refs
    turns = filtered.shape[0]
    n_tile, rows_out, win = out_ref.shape
    me = lax.axis_index("tile")
    classes = n_tile // local
    row_class = lax.rem(me, classes)
    which = lax.div(me, classes)
    proj = lax.axis_index("proj") * local + which
    row_ids = lax.broadcasted_iota(jnp.int32, (rows_out, win), 0)
    row_mod = (row_ids // chunk * classes + row_class) * chunk + row_ids % chunk
    me_y = lax.rem(me, 2)

    step = 2 * local
    near = n_tile // 2 - 1 - len(late_refs)
    for turn in range(n_tile // 2):
        for y in range(2):
            spot = jnp.bitwise_xor(y, me_y) * local + which
            if turn == 0:
                block = own_ref[spot]
            elif turn <= near:
                block = next_ref[step * (turn - 1) + spot]
            else:
                block = late_refs[turn - near - 1][spot]
            table[2 * turn + y] = block

    @pl.loop(0, n_tile, unroll=2)
    def _(k):
        turn = lax.shift_right_logical(k, 1)
        y = jnp.bitwise_and(k, 1)
        col = pl.multiple_of(table[k] * 128, 128)
        tile = lax.rem(me - me_y + 2 * turn, n_tile) + y
        start = start_ref[tile, proj]
        turn_at = lax.shift_right_logical(start, 8)
        later = jnp.minimum(turn_at + 1, turns - 1)
        out_ref[tile] = jnp.where(
            row_mod >= jnp.bitwise_and(start, LMAX - 1),
            filtered[turn_at, :, pl.ds(col, win)],
            filtered[later, :, pl.ds(col, win)],
        )


def spread_sum(recv_ref, rowm_ref, first_ref, colw_ref, out_ref, held, acc, total, sems):
    n_src, rows, win = recv_ref.shape
    local, parts, depth, _ = held.shape
    per = n_src // local

    def fetch(q, k):
        return pltpu.make_async_copy(
            colw_ref.at[q, 0, pl.ds(depth * k, depth)], held.at[q, k], sems.at[q, k]
        )

    for q in range(local):
        for k in range(parts):
            if q:
                fetch(q, k).start()
    for q in range(local):
        for k in range(parts):
            if q:
                fetch(q, k).wait()
            block = held[q, k] if q else first_ref[depth * k : depth * (k + 1)]
            window = recv_ref[per * q : per * (q + 1), :, depth * k : depth * (k + 1)]
            piece = jnp.dot(
                window.reshape(per * rows, depth), block, preferred_element_type=jnp.float32
            )
            if k:
                piece = acc[...] + piece
            if k < parts - 1:
                acc[...] = piece
                continue
            term = jnp.dot(rowm_ref[q], piece.astype(BF16), preferred_element_type=jnp.float32)
            if q:
                term = total[...] + term
            if q < local - 1:
                total[...] = term
            else:
                out_ref[...] = term.reshape(out_ref.shape).astype(BF16)


def body(raw, row_weights, col_weights, band_start, band_length, col_offset):
    proj_count, rows_dev, cols_dev = raw.shape
    n_proj = lax.axis_size("proj")
    n_tile = lax.axis_size("tile")
    proj_me = lax.axis_index("proj")
    tile_me = lax.axis_index("tile")
    local = proj_count // n_proj
    total_rows = rows_dev * n_proj
    total_cols = cols_dev * n_tile
    classes = n_tile // local
    chunk = rows_dev // classes
    slices, vox = row_weights.shape[2], col_weights.shape[3]
    win = col_weights.shape[2]
    rows_out = LMAX // classes

    recv = lax.all_to_all(
        raw.reshape(n_proj * n_tile, chunk, cols_dev),
        ("proj", "tile"),
        split_axis=0,
        concat_axis=0,
        tiled=True,
    ).reshape(n_proj, n_tile, chunk, cols_dev)

    own, ahead, late = gather_offsets(col_offset, n_tile)
    row_class = tile_me % classes
    first_proj = proj_me * local
    starts_all = lax.dynamic_slice(band_start, (first_proj, 0), (local, n_tile))
    lengths_all = lax.dynamic_slice(band_length, (first_proj, 0), (local, n_tile))

    dist = 2.0 * total_cols
    row_ids = (
        rows_dev * jnp.arange(n_proj, dtype=jnp.int32)[:, None]
        + chunk * row_class
        + jnp.arange(chunk, dtype=jnp.int32)[None, :]
    ).astype(jnp.float32)
    vcoord = row_ids + 0.5 - total_rows / 2.0
    ucoord = jnp.arange(total_cols, dtype=jnp.int32).astype(jnp.float32) + 0.5 - total_cols / 2.0
    weight = dist / jnp.sqrt(dist * dist + ucoord[None, None, :] ** 2 + vcoord[:, :, None] ** 2)

    place = jnp.arange(LMAX, dtype=jnp.int32)
    row_mod = place // rows_out * chunk + place % rows_out // chunk * rows_dev + place % chunk
    my_start = lax.dynamic_slice_in_dim(starts_all, tile_me, 1, 1)
    my_length = lax.dynamic_slice_in_dim(lengths_all, tile_me, 1, 1)
    band_row = jnp.bitwise_and(row_mod[None, :] - my_start, LMAX - 1)
    pick = (place[None, :, None] == band_row[:, None, :]) & (band_row < my_length)[:, None, :]
    row_moved = jnp.einsum(
        "qsi,qik->qsk", row_weights[:, 0], pick.astype(BF16), preferred_element_type=jnp.float32
    ).astype(BF16)

    parts = 2
    first = col_weights[0, 0]
    own, row_moved, first = lax.optimization_barrier((own, row_moved, first))
    filtered = pl.pallas_call(
        filter_rows,
        out_shape=jax.ShapeDtypeStruct((total_rows // LMAX, rows_out, total_cols), BF16),
        in_specs=[pl.BlockSpec(memory_space=pltpu.VMEM)] * 3,
        out_specs=pl.BlockSpec(memory_space=pltpu.VMEM),
        scratch_shapes=[pltpu.VMEM((n_proj * chunk, total_cols + 2 * TAP_REACH), BF16)],
        compiler_params=pltpu.CompilerParams(vmem_limit_bytes=24 << 20),
    )(recv, weight, tap_matrix(cols_dev))
    cut = pl.pallas_call(
        functools.partial(cut_windows, local, chunk),
        out_shape=jax.ShapeDtypeStruct((n_tile, rows_out, win), BF16),
        in_specs=[pl.BlockSpec(memory_space=pltpu.SMEM)] * (3 + len(late))
        + [pl.BlockSpec(memory_space=pltpu.VMEM)],
        out_specs=pl.BlockSpec(memory_space=pltpu.VMEM),
        scratch_shapes=[pltpu.SMEM((n_tile,), jnp.int32)],
        compiler_params=pltpu.CompilerParams(vmem_limit_bytes=24 << 20),
    )(band_start.T, own, ahead, *late, filtered)

    windows = lax.all_to_all(cut, "tile", split_axis=0, concat_axis=0, tiled=True)

    part = pl.pallas_call(
        spread_sum,
        out_shape=jax.ShapeDtypeStruct((n_proj, slices // n_proj, vox), BF16),
        in_specs=[
            pl.BlockSpec(memory_space=pltpu.VMEM),
            pl.BlockSpec(memory_space=pltpu.VMEM),
            pl.BlockSpec(memory_space=pltpu.VMEM),
            pl.BlockSpec(memory_space=pl.ANY),
        ],
        out_specs=pl.BlockSpec(memory_space=pltpu.VMEM),
        scratch_shapes=[
            pltpu.VMEM((local, parts, win // parts, vox), BF16),
            pltpu.VMEM((LMAX, vox), jnp.float32),
            pltpu.VMEM((slices, vox), jnp.float32),
            pltpu.SemaphoreType.DMA((local, parts)),
        ],
        compiler_params=pltpu.CompilerParams(vmem_limit_bytes=48 << 20),
    )(windows, row_moved, first, col_weights)

    terms = lax.all_to_all(part, "proj", split_axis=0, concat_axis=0, tiled=True)
    return jnp.sum(terms.astype(jnp.float32), axis=0)


def solution(mesh):
    return jax.shard_map(
        body,
        mesh=mesh,
        in_specs=(
            P(None, "proj", "tile"),
            P("proj", "tile", None, None),
            P("proj", "tile", None, None),
            P(),
            P(),
            P("proj", "tile"),
        ),
        out_specs=P("proj", "tile"),
        check_vma=False,
    )
```

```python
import functools
import math

import jax
import jax.numpy as jnp
from jax import lax
from jax.experimental import pallas as pl
from jax.experimental.pallas import tpu as pltpu
from jax.sharding import PartitionSpec as P

LMAX = 256
TAP_REACH = 128
BF16 = jnp.bfloat16


def tap_matrix(width):
    rows = jnp.arange(width + 2 * TAP_REACH, dtype=jnp.int32)[:, None]
    cols = jnp.arange(width, dtype=jnp.int32)[None, :]
    offset = cols - rows + TAP_REACH
    offset_f = offset.astype(jnp.float32)
    safe_sq = jnp.where(offset == 0, 1.0, offset_f * offset_f)
    value = jnp.where(
        offset == 0, 0.25, jnp.where(offset % 2 != 0, -1.0 / (math.pi * math.pi * safe_sq), 0.0)
    )
    value = jnp.where((offset >= -TAP_REACH) & (offset < TAP_REACH), value, 0.0)
    return value.astype(BF16)


def gather_offsets(offsets, count):
    half = count // 4
    flat = offsets.reshape(-1)
    held = jnp.concatenate([flat, lax.ppermute(flat, "tile", [(i, i ^ 1) for i in range(count)])])
    held = lax.optimization_barrier(held)
    far = [
        lax.ppermute(
            held, "tile", [((i + 2 * (k + half * (i % 2))) % count, i) for i in range(count)]
        )
        for k in range(1, half + 1)
    ]
    mine = lax.optimization_barrier(jnp.concatenate(far))
    return held, mine, lax.ppermute(mine, "tile", [(i, i ^ 1) for i in range(count)])


def filter_rows(recv_ref, weight_ref, taps_ref, out_ref, padded):
    groups, n_src, chunk, width = recv_ref.shape
    rows = groups * chunk
    total = n_src * width
    zero = jnp.zeros((rows, TAP_REACH), BF16)
    padded[:, :TAP_REACH] = zero
    padded[:, TAP_REACH + total :] = zero
    for src in range(n_src):
        lo = width * src
        piece = recv_ref[:, src].astype(jnp.float32) * weight_ref[:, :, lo : lo + width]
        padded[:, lo + TAP_REACH : lo + TAP_REACH + width] = piece.reshape(rows, width).astype(BF16)
    for src in range(n_src):
        lo = width * src
        block = jnp.dot(
            padded[:, lo : lo + width + 2 * TAP_REACH],
            taps_ref[...],
            preferred_element_type=jnp.float32,
        )
        turns, high, _ = out_ref.shape
        out_ref[:, :, lo : lo + width] = block.reshape(turns, high, width).astype(BF16)


def cut_windows(local, chunk, start_ref, own_ref, mine_ref, other_ref, filtered, out_ref):
    turns = filtered.shape[0]
    n_tile, rows_out, win = out_ref.shape
    me = lax.axis_index("tile")
    classes = n_tile // local
    row_class = lax.rem(me, classes)
    which = lax.div(me, classes)
    proj = lax.axis_index("proj") * local + which
    row_ids = lax.broadcasted_iota(jnp.int32, (rows_out, win), 0)
    row_mod = (row_ids // chunk * classes + row_class) * chunk + row_ids % chunk
    half = n_tile // 4
    me_y = lax.rem(me, 2)

    @pl.loop(0, n_tile)
    def _(k):
        turn = lax.div(k, 2)
        y = lax.rem(k, 2)
        side = jnp.where(turn > half, 1, 0)
        near = (jnp.bitwise_xor(y, me_y)) * local + which
        block = jnp.where(turn > half, turn - half, jnp.maximum(turn, 1)) - 1
        spot = (2 * block + jnp.bitwise_xor(y, side)) * local + which
        far = jnp.where(side == me_y, mine_ref[spot], other_ref[spot])
        col = pl.multiple_of(jnp.where(turn == 0, own_ref[near], far) * 128, 128)
        tile = lax.rem(me - me_y + 2 * turn, n_tile) + y
        start = start_ref[tile, proj]
        turn_at = lax.shift_right_logical(start, 8)
        later = jnp.minimum(turn_at + 1, turns - 1)
        out_ref[tile] = jnp.where(
            row_mod >= jnp.bitwise_and(start, LMAX - 1),
            filtered[turn_at, :, pl.ds(col, win)],
            filtered[later, :, pl.ds(col, win)],
        )


def spread_sum(recv_ref, rowm_ref, first_ref, colw_ref, out_ref, held, acc, total, sems):
    n_src, rows, win = recv_ref.shape
    local, parts, depth, _ = held.shape
    per = n_src // local

    def fetch(q, k):
        return pltpu.make_async_copy(
            colw_ref.at[q, 0, pl.ds(depth * k, depth)], held.at[q, k], sems.at[q, k]
        )

    for q in range(local):
        for k in range(parts):
            if q:
                fetch(q, k).start()
    for q in range(local):
        for k in range(parts):
            if q:
                fetch(q, k).wait()
            block = held[q, k] if q else first_ref[depth * k : depth * (k + 1)]
            window = recv_ref[per * q : per * (q + 1), :, depth * k : depth * (k + 1)]
            piece = jnp.dot(
                window.reshape(per * rows, depth), block, preferred_element_type=jnp.float32
            )
            if k:
                piece = acc[...] + piece
            if k < parts - 1:
                acc[...] = piece
                continue
            term = jnp.dot(rowm_ref[q], piece.astype(BF16), preferred_element_type=jnp.float32)
            if q:
                term = total[...] + term
            if q < local - 1:
                total[...] = term
            else:
                out_ref[...] = term.reshape(out_ref.shape).astype(BF16)


def body(raw, row_weights, col_weights, band_start, band_length, col_offset):
    proj_count, rows_dev, cols_dev = raw.shape
    n_proj = lax.axis_size("proj")
    n_tile = lax.axis_size("tile")
    proj_me = lax.axis_index("proj")
    tile_me = lax.axis_index("tile")
    local = proj_count // n_proj
    total_rows = rows_dev * n_proj
    total_cols = cols_dev * n_tile
    classes = n_tile // local
    chunk = rows_dev // classes
    slices, vox = row_weights.shape[2], col_weights.shape[3]
    win = col_weights.shape[2]
    rows_out = LMAX // classes

    recv = lax.all_to_all(
        raw.reshape(n_proj * n_tile, chunk, cols_dev),
        ("proj", "tile"),
        split_axis=0,
        concat_axis=0,
        tiled=True,
    ).reshape(n_proj, n_tile, chunk, cols_dev)

    own, mine, other = gather_offsets(col_offset, n_tile)
    row_class = tile_me % classes
    first_proj = proj_me * local
    starts_all = lax.dynamic_slice(band_start, (first_proj, 0), (local, n_tile))
    lengths_all = lax.dynamic_slice(band_length, (first_proj, 0), (local, n_tile))

    dist = 2.0 * total_cols
    row_ids = (
        rows_dev * jnp.arange(n_proj, dtype=jnp.int32)[:, None]
        + chunk * row_class
        + jnp.arange(chunk, dtype=jnp.int32)[None, :]
    ).astype(jnp.float32)
    vcoord = row_ids + 0.5 - total_rows / 2.0
    ucoord = jnp.arange(total_cols, dtype=jnp.int32).astype(jnp.float32) + 0.5 - total_cols / 2.0
    weight = dist / jnp.sqrt(dist * dist + ucoord[None, None, :] ** 2 + vcoord[:, :, None] ** 2)

    place = jnp.arange(LMAX, dtype=jnp.int32)
    row_mod = place // rows_out * chunk + place % rows_out // chunk * rows_dev + place % chunk
    my_start = lax.dynamic_slice_in_dim(starts_all, tile_me, 1, 1)
    my_length = lax.dynamic_slice_in_dim(lengths_all, tile_me, 1, 1)
    band_row = jnp.bitwise_and(row_mod[None, :] - my_start, LMAX - 1)
    pick = (place[None, :, None] == band_row[:, None, :]) & (band_row < my_length)[:, None, :]
    row_moved = jnp.einsum(
        "qsi,qik->qsk", row_weights[:, 0], pick.astype(BF16), preferred_element_type=jnp.float32
    ).astype(BF16)

    parts = 2
    first = col_weights[0, 0]
    other, row_moved, first = lax.optimization_barrier((other, row_moved, first))
    filtered = pl.pallas_call(
        filter_rows,
        out_shape=jax.ShapeDtypeStruct((total_rows // LMAX, rows_out, total_cols), BF16),
        in_specs=[pl.BlockSpec(memory_space=pltpu.VMEM)] * 3,
        out_specs=pl.BlockSpec(memory_space=pltpu.VMEM),
        scratch_shapes=[pltpu.VMEM((n_proj * chunk, total_cols + 2 * TAP_REACH), BF16)],
        compiler_params=pltpu.CompilerParams(vmem_limit_bytes=24 << 20),
    )(recv, weight, tap_matrix(cols_dev))
    cut = pl.pallas_call(
        functools.partial(cut_windows, local, chunk),
        out_shape=jax.ShapeDtypeStruct((n_tile, rows_out, win), BF16),
        in_specs=[pl.BlockSpec(memory_space=pltpu.SMEM)] * 4
        + [pl.BlockSpec(memory_space=pltpu.VMEM)],
        out_specs=pl.BlockSpec(memory_space=pltpu.VMEM),
        compiler_params=pltpu.CompilerParams(vmem_limit_bytes=24 << 20),
    )(band_start.T, own, mine, other, filtered)

    windows = lax.all_to_all(cut, "tile", split_axis=0, concat_axis=0, tiled=True)

    part = pl.pallas_call(
        spread_sum,
        out_shape=jax.ShapeDtypeStruct((n_proj, slices // n_proj, vox), BF16),
        in_specs=[
            pl.BlockSpec(memory_space=pltpu.VMEM),
            pl.BlockSpec(memory_space=pltpu.VMEM),
            pl.BlockSpec(memory_space=pltpu.VMEM),
            pl.BlockSpec(memory_space=pl.ANY),
        ],
        out_specs=pl.BlockSpec(memory_space=pltpu.VMEM),
        scratch_shapes=[
            pltpu.VMEM((local, parts, win // parts, vox), BF16),
            pltpu.VMEM((LMAX, vox), jnp.float32),
            pltpu.VMEM((slices, vox), jnp.float32),
            pltpu.SemaphoreType.DMA((local, parts)),
        ],
        compiler_params=pltpu.CompilerParams(vmem_limit_bytes=48 << 20),
    )(windows, row_moved, first, col_weights)

    terms = lax.all_to_all(part, "proj", split_axis=0, concat_axis=0, tiled=True)
    return jnp.sum(terms.astype(jnp.float32), axis=0)


def solution(mesh):
    return jax.shard_map(
        body,
        mesh=mesh,
        in_specs=(
            P(None, "proj", "tile"),
            P("proj", "tile", None, None),
            P("proj", "tile", None, None),
            P(),
            P(),
            P("proj", "tile"),
        ),
        out_specs=P("proj", "tile"),
        check_vma=False,
    )
```
